256 devices in a mesh: field: 8 (over y, x_lo), azim: 32 (over z, x_hi, core).
Axes of the slice: x: 4 (x_hi: 2, x_lo: 2; x = x_hi * 2 + x_lo), y: 4, z: 8, core: 2. Of those that a mesh axis runs over, the one named last changes fastest.
Arguments:
- scalars: float32 [64, 10, 512, 1024], P('field', None, 'azim'), may hold values from -5 to 5
- wiener: float32 [64, 512, 1024], P('field', 'azim'), may hold values from -1.2 to 1.2
- velocity: float32 [512, 1024], P('azim', 'field'), may hold values from 0.5 to 2
- diffusivity: float32 [512, 1024], P('azim', 'field'), may hold values from 0.1 to 0.8
- mix_rate: float32 [512, 1024], P('azim', 'field'), may hold values from 0.5 to 4
- reaction_rate: float32 [10], replicated, may hold values from 0.2 to 1.5
- equilibrium: float32 [10], replicated, may hold values from -3 to 3
Outputs:
- advanced: float32 [64, 10, 512, 1024], P('field', None, 'azim')
- density: float32 [512, 1024], P('azim', 'field')
The draws below stay inside these ranges and needn't reach their ends.
All inputs are finite; a program needn't handle non-finite values.
Results may differ from the reference program's by a relative error of at most 0.00002.
Values sent between devices are 32-bit elements; how exact they have to be, the bound alone decides.
A program may use at most 128 MiB of HBM per device.

```python
import math
import jax
import jax.numpy as jnp
from jax import lax

NF = 64
NS = 10
CELLS = 1024
NAZ = 512


def levels(key, dims, pieces, low, top_value):
    factor_of = 1.0
    for dim, blocks in pieces:
        heights = jax.random.uniform(jax.random.fold_in(jax.random.fold_in(key, 6), dim), (blocks,), jnp.float32, low / len(pieces), top_value / len(pieces))
        factor_of = factor_of * jnp.repeat(jnp.exp(heights), dims[dim] // blocks).reshape((-1,) + (1,) * (len(dims) - 1 - dim))
    return factor_of


def noise(rng, shape, spread, bound, shards=(), kind=jnp.bfloat16):
    factor_of = levels(rng, shape, shards, -0.22, 0.18) if shards else 1.0
    values = jax.random.normal(rng, shape, jnp.float32) * spread * factor_of
    return jnp.minimum(jnp.maximum(values, -bound), bound).astype(kind)


def setup_inputs(seed: int = 0) -> dict:
    keys = jax.random.split(jax.random.key(seed), 8)
    return {
        "scalars": noise(keys[0], (NF, NS, NAZ, CELLS), 1.0, 5.0, ((0, 8), (2, 32)), jnp.float32),
        "wiener": noise(keys[1], (NF, NAZ, CELLS), 0.3, 1.2, ((0, 8), (1, 32)), jnp.float32),
        "velocity": jnp.clip(0.5 + 1.5 * jax.random.uniform(keys[2], (NAZ, CELLS), jnp.float32) ** levels(keys[2], (NAZ, CELLS), ((0, 32), (1, 8)), -0.2, 0.2), 0.5, 2.0),
        "diffusivity": jnp.clip(0.1 + 0.7 * jax.random.uniform(keys[3], (NAZ, CELLS), jnp.float32) ** levels(keys[3], (NAZ, CELLS), ((0, 32), (1, 8)), -0.2, 0.2), 0.1, 0.8),
        "mix_rate": jnp.clip(jnp.exp(math.log(4.0) - 2.0794415 * jax.random.uniform(keys[4], (NAZ, CELLS), jnp.float32) ** levels(keys[4], (NAZ, CELLS), ((0, 32), (1, 8)), -0.2, 0.2)), 0.5, 4.0),
        "reaction_rate": jnp.clip(jnp.exp(jax.random.uniform(keys[5], (NS,), jnp.float32, math.log(0.2), math.log(1.5))), 0.2, 1.5),
        "equilibrium": noise(keys[6], (NS,), 1.0, 3.0, (), jnp.float32),
    }


step_size = 0.2

def advance(middle, upper_row, lower_row, velocity, diffusivity, mix_rate, wiener, average, reaction_rate, equilibrium):
    gradient = 0.5 * (upper_row - lower_row)
    laplacian = upper_row - 2.0 * middle + lower_row
    heating = 1.0 + 0.5 * middle[:, 0] * middle[:, 0]
    burning = jnp.exp(1.0 - 1.0 / heating)
    source = reaction_rate[None, :, None, None] * burning[:, None] * (equilibrium[None, :, None, None] - middle)
    tendency = -velocity * gradient + diffusivity * laplacian - 0.5 * mix_rate * (middle - average) + source
    return middle + step_size * tendency + jnp.sqrt(2.0 * diffusivity) * gradient * wiener[:, None]

def run_segment(state, velocity, diffusivity, mix_rate, wiener, reaction_rate, equilibrium):
    average = lax.optimization_barrier(jnp.sum(state, axis=0)) / NF
    upper_row = jnp.roll(state, -1, axis=2)
    lower_row = jnp.roll(state, 1, axis=2)
    return advance(state, upper_row, lower_row, velocity, diffusivity, mix_rate, wiener, average, reaction_rate, equilibrium)

def reference(scalars, wiener, velocity, diffusivity, mix_rate, reaction_rate, equilibrium):
    segment_one = run_segment(scalars, velocity, diffusivity, mix_rate, wiener, reaction_rate, equilibrium)
    advanced = 0.5 * scalars + 0.5 * run_segment(segment_one, velocity, diffusivity, mix_rate, wiener, reaction_rate, equilibrium)
    heating = 1.0 + 0.5 * advanced[:, 0] * advanced[:, 0]
    density = 1.0 / (lax.optimization_barrier(jnp.sum(heating, axis=0)) / NF)
    return (advanced, density)
```

```python
import functools

import jax
import jax.numpy as jnp
from jax import lax
from jax.experimental import pallas as pl
from jax.experimental.pallas import tpu as pltpu
from jax.sharding import PartitionSpec as P

MESH = pl.DeviceIdType.MESH
NF = 64
DT = 0.2
FL = 8
NS = 10
ROWS = 16
CELLS = 1024
QUARTER = 256
CHUNK = 128
HALF = NS // 2


def kernel(
    n_az,
    q_in, w_in, vel_in, dif_in, mix_in, rate, equil,
    adv_out, den_out,
    q, u, w, gas, gas_own, h1, h2, sums, got1, got2, got3, total, e2, heat, heat_got,
    load_sem, out_sem, gas_s, gas_r, h1_s, h1_r, h2_s, h2_r, red_s, red_r, den_s, den_r,
):
    f = lax.axis_index("field")
    a = lax.axis_index("azim")
    y, xl = f // 2, f % 2
    yp, yo, ym = (y + 1) % 4, (y + 2) % 4, (y + 3) % 4
    dev_p, dev_m, dev_x = (yp * 2 + xl, a), (ym * 2 + xl, a), (y * 2 + 1 - xl, a)
    dev_up, dev_dn = (f, (a + 1) % n_az), (f, (a + n_az - 1) % n_az)

    def peer(k):
        return ((f + k) % 8, a)

    def chunk(i):
        return pl.ds(pl.multiple_of(i * CHUNK, CHUNK), CHUNK)

    def quarter(i):
        return pl.ds(pl.multiple_of(i * QUARTER, QUARTER), QUARTER)

    def remote(src, dst, send, recv, device):
        return pltpu.make_async_remote_copy(
            src_ref=src, dst_ref=dst, send_sem=send, recv_sem=recv,
            device_id=device, device_id_type=MESH,
        )

    loads = [pltpu.make_async_copy(q_in.at[i], q.at[i], load_sem.at[i]) for i in range(FL)]
    gas_loads = [
        pltpu.make_async_copy(r, gas_own.at[i], load_sem.at[FL + 1 + i])
        for i, r in enumerate((vel_in, dif_in, mix_in))
    ]
    w_load = pltpu.make_async_copy(w_in, w, load_sem.at[FL])
    for c in gas_loads + loads + [w_load]:
        c.start()

    barrier = pltpu.get_barrier_semaphore()
    greeted = [peer(k) for k in range(1, 8)] + [dev_up, dev_dn]
    for d in greeted:
        pl.semaphore_signal(barrier, inc=1, device_id=d, device_id_type=MESH)
    pl.semaphore_wait(barrier, len(greeted))

    halo1 = [
        remote(q_in.at[:, :, pl.ds(ROWS - 1, 1), :], h1.at[0], h1_s.at[0], h1_r.at[0], dev_up),
        remote(q_in.at[:, :, pl.ds(0, 1), :], h1.at[1], h1_s.at[1], h1_r.at[1], dev_dn),
    ]
    for c in gas_loads:
        c.wait()
    gas_sends = [
        remote(gas_own, gas.at[:, :, chunk(f)], gas_s.at[k], gas_r.at[k], peer(k + 1))
        for k in range(7)
    ]
    for c in gas_sends:
        c.start()
    for c in halo1:
        c.start()
    gas[:, :, chunk(f)] = gas_own[...]
    for c in loads:
        c.wait()

    def red(n, i, src, dst, device):
        return remote(src, dst, red_s.at[n, i], red_r.at[n, i], device)

    lo, hi = pl.ds(0, HALF), pl.ds(HALF, HALF)

    def step1(n):
        return [
            red(n, 0, sums.at[n, lo, :, quarter(yo)], got1.at[n, 0], dev_p),
            red(n, 1, sums.at[n, hi, :, quarter(yo)], got1.at[n, 1], dev_m),
        ]

    def step2a(n):
        return [
            red(n, 2, sums.at[n, hi, :, quarter(yp)], got2.at[n, 0, hi], dev_p),
            red(n, 3, sums.at[n, lo, :, quarter(ym)], got2.at[n, 1, lo], dev_m),
        ]

    def step2b(n):
        return [
            red(n, 4, sums.at[n, lo, :, quarter(yp)], got2.at[n, 0, lo], dev_p),
            red(n, 5, sums.at[n, hi, :, quarter(ym)], got2.at[n, 1, hi], dev_m),
        ]

    def step3(n):
        return red(n, 6, sums.at[n, :, :, chunk(y * 2 + 1 - xl)], got3.at[n], dev_x)

    def gather_own(n):
        piece = total.at[n, :, :, chunk(f)]
        return [red(n, 7, piece, piece, dev_x), red(n, 8, piece, piece, dev_p), red(n, 9, piece, piece, dev_m)]

    def gather_x(n):
        piece = total.at[n, :, :, chunk(y * 2 + 1 - xl)]
        return [red(n, 10, piece, piece, dev_p), red(n, 11, piece, piece, dev_m)]

    def pass_on(n, which):
        side = xl if which == 0 else 1 - xl
        from_m = total.at[n, lo, :, chunk(ym * 2 + side)]
        from_p = total.at[n, hi, :, chunk(yp * 2 + side)]
        return [
            red(n, 12 + 2 * which, from_m, from_m, dev_p),
            red(n, 13 + 2 * which, from_p, from_p, dev_m),
        ]

    def start(copies):
        for c in copies:
            c.start()

    def arrive(copies):
        for c in copies:
            c.wait_recv()

    def after1(n):
        arrive(step1(n))

        def body(s, _):
            sums[n, s, :, quarter(yp)] += got1[n, 0, s]
            sums[n, HALF + s, :, quarter(ym)] += got1[n, 1, s]
            return 0

        lax.fori_loop(0, HALF, body, 0)
        start(step2b(n))

    def after2(n):
        arrive(step2a(n) + step2b(n))

        def body(s, _):
            sums[n, s, :, quarter(y)] += got2[n, 0, s] + got2[n, 1, s]
            return 0

        lax.fori_loop(0, NS, body, 0)
        step3(n).start()

    def after3(n):
        step3(n).wait_recv()

        def body(s, _):
            total[n, s, :, chunk(f)] = sums[n, s, :, chunk(f)] + got3[n, s]
            return 0

        lax.fori_loop(0, NS, body, 0)
        start(gather_own(n))

    def after_x(n):
        gather_own(n)[0].wait_recv()
        start(gather_x(n))

    def after_own(n):
        arrive(gather_own(n)[1:])
        start(pass_on(n, 0))

    def after_partner(n):
        arrive(gather_x(n))
        start(pass_on(n, 1))

    def after_all(n):
        arrive(pass_on(n, 0) + pass_on(n, 1))

    def sum_q(k):
        def body(s, _):
            acc = q[0, s, :, quarter(k)]
            for i in range(1, FL):
                acc = acc + q[i, s, :, quarter(k)]
            sums[0, s, :, quarter(k)] = acc
            return 0

        lax.fori_loop(0, NS, body, 0)

    sum_q(yo)
    start(step1(0))
    sum_q(yp)
    step2a(0)[0].start()
    sum_q(ym)
    step2a(0)[1].start()
    sum_q(y)
    after1(0)

    row = lax.broadcasted_iota(jnp.int32, (8, CHUNK), 0)
    first, last = row == 0, row == 7
    tiles = (pl.ds(0, 8), pl.ds(8, 8))

    def neighbours(lower, upper, below, above):
        lower_up, upper_up = pltpu.roll(lower, 7, 0), pltpu.roll(upper, 7, 0)
        lower_dn, upper_dn = pltpu.roll(lower, 1, 0), pltpu.roll(upper, 1, 0)
        up = (jnp.where(last, upper_up, lower_up), jnp.where(last, above, upper_up))
        dn = (jnp.where(first, below, lower_dn), jnp.where(first, lower_dn, upper_dn))
        return up, dn

    def coefficients(cols, t):
        vel, dif, mix = gas[0, tiles[t], cols], gas[1, tiles[t], cols], gas[2, tiles[t], cols]
        keep = 1.0 - (2.0 * DT) * dif - (0.5 * DT) * mix
        return keep, DT * dif, (-0.5 * DT) * vel, 0.5 * jnp.sqrt(2.0 * dif)

    def burn(x):
        heating = 1.0 + 0.5 * x * x
        return DT * jnp.exp(1.0 - 1.0 / heating)

    def explicit(k):
        def column(j, _):
            cols = chunk(k * 2 + j)
            co = [coefficients(cols, t) for t in range(2)]

            def field(i, acc):
                grad_c = [co[t][2] + co[t][3] * w[i, tiles[t], cols] for t in range(2)]
                b = [burn(q[i, 0, tiles[t], cols]) for t in range(2)]
                out = []
                for s in range(NS):
                    x = [q[i, s, tiles[t], cols] for t in range(2)]
                    below = jnp.broadcast_to(h1[0, i, s, :, cols], (8, CHUNK))
                    above = jnp.broadcast_to(h1[1, i, s, :, cols], (8, CHUNK))
                    up, dn = neighbours(x[0], x[1], below, above)
                    for t in range(2):
                        v = (
                            x[t] * co[t][0]
                            + (up[t] - dn[t]) * grad_c[t]
                            + (up[t] + dn[t]) * co[t][1]
                            + (rate[s] * b[t]) * (equil[s] - x[t])
                        )
                        u[i, s, tiles[t], cols] = v
                        out.append(acc[2 * s + t] + v)
                return tuple(out)

            acc = lax.fori_loop(0, FL, field, (jnp.zeros((8, CHUNK), jnp.float32),) * (2 * NS))
            for s in range(NS):
                for t in range(2):
                    sums[1, s, tiles[t], cols] = acc[2 * s + t]
            return 0

        lax.fori_loop(0, 2, column, 0)

    after2(0)
    arrive(gas_sends)
    w_load.wait()
    arrive(halo1)
    explicit(yo)
    start(step1(1))
    after3(0)
    explicit(yp)
    step2a(1)[0].start()
    after_x(0)
    explicit(ym)
    step2a(1)[1].start()
    explicit(y)
    after1(1)
    after_own(0)
    after_partner(0)

    def halo2(k, i):
        cols = quarter(k)
        return [
            remote(u.at[:, :, pl.ds(ROWS - 1, 1), cols], h2.at[0, :, :, :, cols], h2_s.at[0, i], h2_r.at[0, i], dev_up),
            remote(u.at[:, :, pl.ds(0, 1), cols], h2.at[1, :, :, :, cols], h2_s.at[1, i], h2_r.at[1, i], dev_dn),
        ]

    def mixed(k, n):
        def body(s, _):
            cols = quarter(k)
            e = (0.5 * DT / NF) * gas[2, :, cols] * total[0, s, :, cols]
            for i in range(FL):
                u[i, s, :, cols] += e
            return 0

        lax.fori_loop(0, NS, body, 0)
        start(halo2(k, n))

    mixed(y, 0)
    after2(1)
    mixed(ym, 1)
    mixed(yp, 2)
    after3(1)
    after_all(0)
    mixed(yo, 3)
    after_x(1)

    def second(k, n):
        cols_q = quarter(k)

        def column(j, _):
            cols = chunk(k * 2 + j)
            co = [coefficients(cols, t) for t in range(2)]
            for s in range(NS):
                for t in range(2):
                    m = (0.5 * DT) * gas[2, tiles[t], cols]
                    first_mean = m * total[0, s, tiles[t], cols]
                    e2[s, tiles[t], :] = (0.5 / NF) * m * (total[1, s, tiles[t], cols] + first_mean)
            half = [tuple(0.5 * c for c in co[t]) for t in range(2)]

            def field(i, acc):
                grad_c = [half[t][2] + half[t][3] * w[i, tiles[t], cols] for t in range(2)]
                b = [0.5 * burn(u[i, 0, tiles[t], cols]) for t in range(2)]
                out = list(acc)
                for s in range(NS):
                    x = [u[i, s, tiles[t], cols] for t in range(2)]
                    below = jnp.broadcast_to(h2[0, i, s, :, cols], (8, CHUNK))
                    above = jnp.broadcast_to(h2[1, i, s, :, cols], (8, CHUNK))
                    up, dn = neighbours(x[0], x[1], below, above)
                    for t in range(2):
                        v = (
                            0.5 * q[i, s, tiles[t], cols]
                            + x[t] * half[t][0]
                            + (up[t] - dn[t]) * grad_c[t]
                            + (up[t] + dn[t]) * half[t][1]
                            + e2[s, tiles[t], :]
                            + (rate[s] * b[t]) * (equil[s] - x[t])
                        )
                        q[i, s, tiles[t], cols] = v
                        if s == 0:
                            out[t] = out[t] + (1.0 + 0.5 * v * v)
                return tuple(out)

            acc = lax.fori_loop(0, FL, field, (jnp.zeros((8, CHUNK), jnp.float32),) * 2)
            for t in range(2):
                heat[tiles[t], cols] = acc[t]
            return 0

        for c in halo2(k, n):
            c.wait_recv()
        lax.fori_loop(0, 2, column, 0)

    def write(k, n):
        cols = quarter(k)
        return pltpu.make_async_copy(q.at[:, :, :, cols], adv_out.at[:, :, :, cols], out_sem.at[n])

    def den(k, n):
        out = []
        for side in range(2):
            owner = k * 2 + (xl + side) % 2
            out.append(
                remote(heat.at[:, chunk(owner)], heat_got.at[n, side], den_s.at[n, side], den_r.at[n, side], (owner, a))
            )
        return out

    second(y, 0)
    den(y, 0)[1].start()
    write(y, 0).start()
    after_own(1)
    after_partner(1)
    second(ym, 1)
    start(den(ym, 1))
    write(ym, 1).start()
    second(yp, 2)
    start(den(yp, 2))
    write(yp, 2).start()
    after_all(1)
    second(yo, 3)
    start(den(yo, 3))
    write(yo, 3).start()

    heat_sum = heat[:, chunk(f)]
    den(y, 0)[1].wait_recv()
    heat_sum = heat_sum + heat_got[0, 1]
    for n, k in ((1, ym), (2, yp), (3, yo)):
        arrive(den(k, n))
        heat_sum = heat_sum + heat_got[n, 0] + heat_got[n, 1]
    den_out[...] = 1.0 / (heat_sum * (1.0 / NF))

    for c in gas_sends + halo1:
        c.wait_send()
    for n in range(2):
        copies = step1(n) + step2a(n) + step2b(n) + [step3(n)] + gather_own(n) + gather_x(n) + pass_on(n, 0) + pass_on(n, 1)
        for c in copies:
            c.wait_send()
    den(y, 0)[1].wait_send()
    for n, k in ((0, y), (1, ym), (2, yp), (3, yo)):
        for c in halo2(k, n):
            c.wait_send()
        if n:
            for c in den(k, n):
                c.wait_send()
        write(k, n).wait()


def solution(mesh):
    n_az = mesh.shape["azim"]

    def shards(scalars, wiener, velocity, diffusivity, mix_rate, reaction_rate, equilibrium):
        any_ = pl.BlockSpec(memory_space=pl.ANY)
        smem = pl.BlockSpec(memory_space=pltpu.SMEM)
        f32 = jnp.float32
        dma = pltpu.SemaphoreType.DMA
        return pl.pallas_call(
            functools.partial(kernel, n_az),
            out_shape=(
                jax.ShapeDtypeStruct((FL, NS, ROWS, CELLS), f32),
                jax.ShapeDtypeStruct((ROWS, CHUNK), f32),
            ),
            in_specs=[any_] * 5 + [smem] * 2,
            out_specs=(any_, pl.BlockSpec(memory_space=pltpu.VMEM)),
            scratch_shapes=[
                pltpu.VMEM((FL, NS, ROWS, CELLS), f32),
                pltpu.VMEM((FL, NS, ROWS, CELLS), f32),
                pltpu.VMEM((FL, ROWS, CELLS), f32),
                pltpu.VMEM((3, ROWS, CELLS), f32),
                pltpu.VMEM((3, ROWS, CHUNK), f32),
                pltpu.VMEM((2, FL, NS, 1, CELLS), f32),
                pltpu.VMEM((2, FL, NS, 1, CELLS), f32),
                pltpu.VMEM((2, NS, ROWS, CELLS), f32),
                pltpu.VMEM((2, 2, HALF, ROWS, QUARTER), f32),
                pltpu.VMEM((2, 2, NS, ROWS, QUARTER), f32),
                pltpu.VMEM((2, NS, ROWS, CHUNK), f32),
                pltpu.VMEM((2, NS, ROWS, CELLS), f32),
                pltpu.VMEM((NS, ROWS, CHUNK), f32),
                pltpu.VMEM((ROWS, CELLS), f32),
                pltpu.VMEM((4, 2, ROWS, CHUNK), f32),
                dma((FL + 4,)), dma((4,)),
                dma((7,)), dma((7,)),
                dma((2,)), dma((2,)),
                dma((2, 4)), dma((2, 4)),
                dma((2, 16)), dma((2, 16)),
                dma((4, 2)), dma((4, 2)),
            ],
            compiler_params=pltpu.CompilerParams(
                collective_id=0, has_side_effects=True, vmem_limit_bytes=48 << 20
            ),
            name="fields_step",
        )(scalars, wiener, velocity, diffusivity, mix_rate, reaction_rate, equilibrium)

    return jax.shard_map(
        shards,
        mesh=mesh,
        in_specs=(
            P("field", None, "azim", None),
            P("field", "azim", None),
            P("azim", "field"),
            P("azim", "field"),
            P("azim", "field"),
            P(),
            P(),
        ),
        out_specs=(P("field", None, "azim", None), P("azim", "field")),
        check_vma=False,
    )
```

```python
import functools

import jax
import jax.numpy as jnp
from jax import lax
from jax.experimental import pallas as pl
from jax.experimental.pallas import tpu as pltpu
from jax.sharding import PartitionSpec as P

MESH = pl.DeviceIdType.MESH
loop = lax.fori_loop
NF = 64
DT = 0.2
FL = 8
NS = 10
ROWS = 16
CELLS = 1024
QUARTER = 256
CHUNK = 128
HALF = NS // 2


def kernel(
    n_az,
    q_in, w_in, vel_in, dif_in, mix_in, rate_in, equil_in,
    adv_out, den_out,
    q, u, w, gas, gas_own, h1, h2, eh, sums, got, got_x, total, corr, corr_got, e1, e2, heat, heat_got, rate, equil,
    load_sem, gas_s, gas_r, h1_s, h1_r, h2_s, h2_r, eh_s, eh_r, red_s, red_r, cor_s, cor_r, den_s, den_r,
):
    f = lax.axis_index("field")
    a = lax.axis_index("azim")
    y, xl = f // 2, f % 2
    yp, yo, ym = (y + 1) % 4, (y + 2) % 4, (y + 3) % 4
    dev_p, dev_m, dev_o, dev_x = (yp * 2 + xl, a), (ym * 2 + xl, a), (yo * 2 + xl, a), (y * 2 + 1 - xl, a)
    around = ((yo, dev_o), (yp, dev_p), (ym, dev_m))
    dev_up, dev_dn = (f, (a + 1) % n_az), (f, (a + n_az - 1) % n_az)

    def peer(k):
        return (f + k) % 8

    def chunk(i):
        return pl.ds(pl.multiple_of(i * CHUNK, CHUNK), CHUNK)

    def quarter(i):
        return pl.ds(pl.multiple_of(i * QUARTER, QUARTER), QUARTER)

    def remote(src, dst, send, recv, device):
        return pltpu.make_async_remote_copy(
            src_ref=src, dst_ref=dst, send_sem=send, recv_sem=recv,
            device_id=device, device_id_type=MESH,
        )

    def start(copies):
        for c in copies:
            c.start()

    def arrive(copies):
        for c in copies:
            c.wait_recv()

    loads = [pltpu.make_async_copy(q_in.at[i], q.at[i], load_sem.at[i]) for i in range(FL)]
    gas_loads = [
        pltpu.make_async_copy(r, gas_own.at[i], load_sem.at[FL + 1 + i])
        for i, r in enumerate((vel_in, dif_in, mix_in))
    ]
    other_loads = [
        pltpu.make_async_copy(w_in, w, load_sem.at[FL]),
        pltpu.make_async_copy(rate_in, rate, load_sem.at[FL + 4]),
        pltpu.make_async_copy(equil_in, equil, load_sem.at[FL + 5]),
    ]

    barrier = pltpu.get_barrier_semaphore()
    first_slab = 1 - jnp.minimum(a, 1)

    def greet(device):
        pl.semaphore_signal(barrier, inc=1, device_id=device, device_id_type=MESH)

    for k in range(1, 8):
        greet((peer(k), a))
    pl.when(a != n_az - 1)(lambda: greet(dev_up))
    pl.when(a != 0)(lambda: greet(dev_dn))
    for c in gas_loads + loads + other_loads:
        c.start()
    pl.semaphore_wait(barrier, 9 - first_slab)
    pl.when(a == 0)(lambda: greet(dev_dn))
    pl.when(a == n_az - 1)(lambda: greet(dev_up))

    for c in gas_loads:
        c.wait()
    gas_sends = [
        remote(gas_own, gas.at[:, :, chunk(f)], gas_s.at[k], gas_r.at[k], (peer(k + 1), a))
        for k in range(7)
    ]
    start(gas_sends)
    gas[:, :, chunk(f)] = gas_own[...]

    halo1 = [
        remote(q_in.at[:, :, pl.ds(ROWS - 1, 1), :], h1.at[0], h1_s.at[0], h1_r.at[0], dev_up),
        remote(q_in.at[:, :, pl.ds(0, 1), :], h1.at[1], h1_s.at[1], h1_r.at[1], dev_dn),
    ]
    halo1[0].start()
    pl.when(a != 0)(lambda: halo1[1].start())

    def late_halo():
        def send():
            pl.semaphore_wait(barrier, 1)
            halo1[1].start()

        pl.when(a == 0)(send)

    def part(p):
        return pl.ds(p * HALF, HALF)

    def red(n, p, i, src, dst, device):
        return remote(src, dst, red_s.at[n * 2 + p, i], red_r.at[n * 2 + p, i], device)

    def scatter(n, p, i):
        k, device = around[i]
        return red(n, p, i, sums.at[n, part(p), :, quarter(k)], got.at[n, p, i], device)

    def exchange(n, p):
        return red(n, p, 3, sums.at[n, part(p), :, quarter(y)], got_x.at[n, p], dev_x)

    def gather(n, p, i):
        piece = total.at[n, part(p), :, quarter(y)]
        return red(n, p, 4 + i, piece, piece, around[i][1])

    def after_scatter(n, p):
        arrive([scatter(n, p, i) for i in range(3)])

        def add(i, _):
            cols = quarter(y)
            sums[n, p * HALF + i, :, cols] += got[n, p, 0, i] + (got[n, p, 1, i] + got[n, p, 2, i])
            return 0

        loop(0, HALF, add, 0)
        exchange(n, p).start()

    def after_exchange(n, p):
        exchange(n, p).wait_recv()

        def add(i, _):
            for j in range(2):
                cols, part_cols = chunk(2 * y + j), pl.ds(j * CHUNK, CHUNK)
                for t in range(2):
                    v = sums[n, p * HALF + i, tiles[t], cols] + got_x[n, p, i, tiles[t], part_cols]
                    if n == 1:
                        edge = corr[t, p * HALF + i, :, cols]
                        for k in range(7):
                            edge = edge + corr_got[k, t, p * HALF + i, :, part_cols]
                        v = v + jnp.where((first, last)[t], jnp.broadcast_to(edge, (8, CHUNK)), 0.0)
                    total[n, p * HALF + i, tiles[t], cols] = v
            return 0

        loop(0, HALF, add, 0)
        start([gather(n, p, i) for i in range(3)])

    row = lax.broadcasted_iota(jnp.int32, (8, CHUNK), 0)
    first, last = row == 0, row == 7
    tiles = (pl.ds(0, 8), pl.ds(8, 8))

    def sum_q(k):
        def body(s, _):
            acc = q[0, s, :, quarter(k)]
            for i in range(1, FL):
                acc = acc + q[i, s, :, quarter(k)]
            sums[0, s, :, quarter(k)] = acc
            return 0

        loop(0, NS, body, 0)

    for c in loads:
        c.wait()
    for i, (k, _) in enumerate(around):
        sum_q(k)
        start([scatter(0, p, i) for p in range(2)])
    sum_q(y)

    def neighbours(lower, upper, below, above):
        lower_up, upper_up = pltpu.roll(lower, 7, 0), pltpu.roll(upper, 7, 0)
        lower_dn, upper_dn = pltpu.roll(lower, 1, 0), pltpu.roll(upper, 1, 0)
        up = (jnp.where(last, upper_up, lower_up), jnp.where(last, above, upper_up))
        dn = (jnp.where(first, below, lower_dn), jnp.where(first, lower_dn, upper_dn))
        return up, dn

    def coefficients(cols, t):
        vel, dif, mix = gas[0, tiles[t], cols], gas[1, tiles[t], cols], gas[2, tiles[t], cols]
        keep = 1.0 - (2.0 * DT) * dif - (0.5 * DT) * mix
        return keep, DT * dif, (-0.5 * DT) * vel, 0.5 * jnp.sqrt(2.0 * dif)

    def burn(x):
        heating = 1.0 + 0.5 * x * x
        return DT * jnp.exp(1.0 - 1.0 / heating)

    zero = jnp.zeros((8, CHUNK), jnp.float32)

    def explicit(k):
        def column(j, _):
            cols = chunk(k * 2 + j)
            co = [coefficients(cols, t) for t in range(2)]

            def field(i, acc):
                grad_c = [co[t][2] + co[t][3] * w[i, tiles[t], cols] for t in range(2)]
                b = [burn(q[i, 0, tiles[t], cols]) for t in range(2)]
                out = []
                for s in range(NS):
                    x = [q[i, s, tiles[t], cols] for t in range(2)]
                    up, dn = neighbours(x[0], x[1], zero, zero)
                    for t in range(2):
                        v = (
                            x[t] * co[t][0]
                            + (up[t] - dn[t]) * grad_c[t]
                            + (up[t] + dn[t]) * co[t][1]
                            + (rate[s] * b[t]) * (equil[s] - x[t])
                        )
                        u[i, s, tiles[t], cols] = v
                        out.append(acc[2 * s + t] + v)
                return tuple(out)

            acc = loop(0, FL, field, (zero,) * (2 * NS))
            for s in range(NS):
                for t in range(2):
                    sums[1, s, tiles[t], cols] = acc[2 * s + t]
            return 0

        loop(0, 2, column, 0)

    def edges():
        def column(j, _):
            cols = chunk(j)
            co = [coefficients(cols, t) for t in range(2)]

            def field(i, acc):
                grad_c = [co[t][2] + co[t][3] * w[i, tiles[t], cols] for t in range(2)]
                coef = (jnp.where(first, co[0][1] - grad_c[0], 0.0), jnp.where(last, co[1][1] + grad_c[1], 0.0))
                out = []
                for s in range(NS):
                    for t in range(2):
                        v = jnp.broadcast_to(h1[t, i, s, :, cols], (8, CHUNK)) * coef[t]
                        u[i, s, tiles[t], cols] += v
                        out.append(acc[2 * s + t] + v)
                return tuple(out)

            acc = loop(0, FL, field, (zero,) * (2 * NS))
            for s in range(NS):
                corr[0, s, :, cols] = acc[2 * s][0:1]
                corr[1, s, :, cols] = acc[2 * s + 1][7:8]
            return 0

        loop(0, CELLS // CHUNK, column, 0)

    def corrections():
        out = []
        for k in range(7):
            owner = peer(k + 1)
            piece = corr.at[:, :, :, quarter(owner // 2)]
            out.append(remote(piece, corr_got.at[k], cor_s.at[k], cor_r.at[k], (owner, a)))
        return out

    halo2 = [
        remote(u.at[:, :, pl.ds(ROWS - 1, 1), :], h2.at[0], h2_s.at[0], h2_r.at[0], dev_up),
        remote(u.at[:, :, pl.ds(0, 1), :], h2.at[1], h2_s.at[1], h2_r.at[1], dev_dn),
    ]

    def mean_rows(p):
        return [
            remote(e1.at[part(p), pl.ds(ROWS - 1, 1), :], eh.at[0, part(p)], eh_s.at[0, p], eh_r.at[0, p], dev_up),
            remote(e1.at[part(p), pl.ds(0, 1), :], eh.at[1, part(p)], eh_s.at[1, p], eh_r.at[1, p], dev_dn),
        ]

    def mixing(p):
        arrive([gather(0, p, i) for i in range(3)])

        def body(i, _):
            e1[p * HALF + i] = (0.5 * DT / NF) * gas[2] * total[0, p * HALF + i]
            return 0

        loop(0, HALF, body, 0)
        start(mean_rows(p))

    def second(k, scalars):
        def column(j, _):
            cols = chunk(k * 2 + j)
            half = [tuple(0.5 * c for c in coefficients(cols, t)) for t in range(2)]
            for s in scalars:
                for t in range(2):
                    m = (0.25 * DT) * gas[2, tiles[t], cols]
                    e2[s, tiles[t], :] = m * ((1.0 / NF) * total[1, s, tiles[t], cols] + e1[s, tiles[t], cols])

            def field(i, acc):
                grad_c = [half[t][2] + half[t][3] * w[i, tiles[t], cols] for t in range(2)]
                b = [0.5 * burn(u[i, 0, tiles[t], cols] + e1[0, tiles[t], cols]) for t in range(2)]
                out = list(acc)
                for s in scalars:
                    x = [u[i, s, tiles[t], cols] + e1[s, tiles[t], cols] for t in range(2)]
                    below = jnp.broadcast_to(h2[0, i, s, :, cols] + eh[0, s, :, cols], (8, CHUNK))
                    above = jnp.broadcast_to(h2[1, i, s, :, cols] + eh[1, s, :, cols], (8, CHUNK))
                    up, dn = neighbours(x[0], x[1], below, above)
                    for t in range(2):
                        v = (
                            0.5 * q[i, s, tiles[t], cols]
                            + x[t] * half[t][0]
                            + (up[t] - dn[t]) * grad_c[t]
                            + (up[t] + dn[t]) * half[t][1]
                            + e2[s, tiles[t], :]
                            + (rate[s] * b[t]) * (equil[s] - x[t])
                        )
                        adv_out[i, s, tiles[t], cols] = v
                        if s == 0:
                            out[t] = out[t] + (1.0 + 0.5 * v * v)
                return tuple(out)

            acc = loop(0, FL, field, (zero,) * 2)
            if 0 in scalars:
                for t in range(2):
                    heat[tiles[t], cols] = acc[t]
            return 0

        loop(0, 2, column, 0)

    def den(k, n):
        out = []
        for side in range(2 if n else 1):
            owner = k * 2 + ((xl + side) % 2 if n else 1 - xl)
            out.append(
                remote(heat.at[:, chunk(owner)], heat_got.at[n, side], den_s.at[n, side], den_r.at[n, side], (owner, a))
            )
        return out

    arrive(gas_sends)
    for c in other_loads:
        c.wait()
    for i, (k, _) in enumerate(around):
        explicit(k)
        start([scatter(1, p, i) for p in range(2)])
    after_scatter(0, 0)
    after_scatter(0, 1)
    explicit(y)
    late_halo()
    after_exchange(0, 0)
    after_exchange(0, 1)
    arrive(halo1)
    edges()
    start(corrections())
    start(halo2)
    after_scatter(1, 0)
    after_scatter(1, 1)
    arrive(corrections())
    after_exchange(1, 0)
    after_exchange(1, 1)
    mixing(0)
    mixing(1)
    arrive(halo2)
    for p in range(2):
        scalars = tuple(range(p * HALF, p * HALF + HALF))
        arrive(mean_rows(p))
        for n, (k, i) in enumerate(((y, None), (yp, 2), (ym, 1), (yo, 0))):
            if n:
                gather(1, p, i).wait_recv()
            second(k, scalars)
            if p == 0:
                start(den(k, n))

    heat_sum = heat[:, chunk(f)]
    for n, k in enumerate((y, yp, ym, yo)):
        for i, c in enumerate(den(k, n)):
            c.wait_recv()
            heat_sum = heat_sum + heat_got[n, i]
    den_out[...] = 1.0 / (heat_sum * (1.0 / NF))

    for n, k in enumerate((y, yp, ym, yo)):
        for c in den(k, n):
            c.wait_send()
    for c in gas_sends + halo1 + halo2 + mean_rows(0) + mean_rows(1) + corrections():
        c.wait_send()
    for n in range(2):
        for p in range(2):
            for c in [scatter(n, p, i) for i in range(3)] + [exchange(n, p)] + [gather(n, p, i) for i in range(3)]:
                c.wait_send()


def solution(mesh):
    n_az = mesh.shape["azim"]

    def shards(scalars, wiener, velocity, diffusivity, mix_rate, reaction_rate, equilibrium):
        hbm = pl.BlockSpec(memory_space=pltpu.HBM)
        vmem = pl.BlockSpec(memory_space=pltpu.VMEM)
        f32 = jnp.float32
        dma = pltpu.SemaphoreType.DMA
        return pl.pallas_call(
            functools.partial(kernel, n_az),
            out_shape=(
                jax.ShapeDtypeStruct((FL, NS, ROWS, CELLS), f32),
                jax.ShapeDtypeStruct((ROWS, CHUNK), f32),
            ),
            in_specs=[hbm] * 7,
            out_specs=(vmem, vmem),
            scratch_shapes=[
                pltpu.VMEM((FL, NS, ROWS, CELLS), f32),
                pltpu.VMEM((FL, NS, ROWS, CELLS), f32),
                pltpu.VMEM((FL, ROWS, CELLS), f32),
                pltpu.VMEM((3, ROWS, CELLS), f32),
                pltpu.VMEM((3, ROWS, CHUNK), f32),
                pltpu.VMEM((2, FL, NS, 1, CELLS), f32),
                pltpu.VMEM((2, FL, NS, 1, CELLS), f32),
                pltpu.VMEM((2, NS, 1, CELLS), f32),
                pltpu.VMEM((2, NS, ROWS, CELLS), f32),
                pltpu.VMEM((2, 2, 3, HALF, ROWS, QUARTER), f32),
                pltpu.VMEM((2, 2, HALF, ROWS, QUARTER), f32),
                pltpu.VMEM((2, NS, ROWS, CELLS), f32),
                pltpu.VMEM((2, NS, 1, CELLS), f32),
                pltpu.VMEM((7, 2, NS, 1, QUARTER), f32),
                pltpu.VMEM((NS, ROWS, CELLS), f32),
                pltpu.VMEM((NS, ROWS, CHUNK), f32),
                pltpu.VMEM((ROWS, CELLS), f32),
                pltpu.VMEM((4, 2, ROWS, CHUNK), f32),
                pltpu.SMEM((NS,), f32),
                pltpu.SMEM((NS,), f32),
                dma((FL + 6,)),
                dma((7,)), dma((7,)),
                dma((2,)), dma((2,)),
                dma((2,)), dma((2,)),
                dma((2, 2)), dma((2, 2)),
                dma((4, 7)), dma((4, 7)),
                dma((7,)), dma((7,)),
                dma((4, 2)), dma((4, 2)),
            ],
            compiler_params=pltpu.CompilerParams(
                collective_id=0, has_side_effects=True, vmem_limit_bytes=48 << 20
            ),
            name="fields_step",
        )(
            *(
                pltpu.with_memory_space_constraint(x, pltpu.HBM)
                for x in (scalars, wiener, velocity, diffusivity, mix_rate, reaction_rate, equilibrium)
            )
        )

    return jax.shard_map(
        shards,
        mesh=mesh,
        in_specs=(
            P("field", None, "azim", None),
            P("field", "azim", None),
            P("azim", "field"),
            P("azim", "field"),
            P("azim", "field"),
            P(),
            P(),
        ),
        out_specs=(P("field", None, "azim", None), P("azim", "field")),
        check_vma=False,
    )
```

```python
import functools

import jax
import jax.numpy as jnp
from jax import lax
from jax.experimental import pallas as pl
from jax.experimental.pallas import tpu as pltpu
from jax.sharding import PartitionSpec as P

MESH = pl.DeviceIdType.MESH
loop = lax.fori_loop
NF = 64
DT = 0.2
FL = 8
NS = 10
ROWS = 16
CELLS = 1024
QUARTER = 256
CHUNK = 128
HALF = NS // 2


def kernel(
    n_az,
    q_in, w_in, vel_in, dif_in, mix_in, rate_in, equil_in,
    adv_out, den_out,
    q, u, w, gas, gas_own, h1, h2, eh, sums, got, got_x, total, corr, corr_got, e1, e2, heat, heat_got, rate, equil,
    load_sem, gas_s, gas_r, h1_s, h1_r, h2_s, h2_r, eh_s, eh_r, red_s, red_r, cor_s, cor_r, den_s, den_r,
):
    f = lax.axis_index("field")
    a = lax.axis_index("azim")
    y, xl = f // 2, f % 2
    yp, yo, ym = (y + 1) % 4, (y + 2) % 4, (y + 3) % 4
    dev_p, dev_m, dev_o, dev_x = (yp * 2 + xl, a), (ym * 2 + xl, a), (yo * 2 + xl, a), (y * 2 + 1 - xl, a)
    around = ((yo, dev_o), (yp, dev_p), (ym, dev_m))
    dev_up, dev_dn = (f, (a + 1) % n_az), (f, (a + n_az - 1) % n_az)

    def peer(k):
        return (f + k) % 8

    def chunk(i):
        return pl.ds(pl.multiple_of(i * CHUNK, CHUNK), CHUNK)

    def quarter(i):
        return pl.ds(pl.multiple_of(i * QUARTER, QUARTER), QUARTER)

    def remote(src, dst, send, recv, device):
        return pltpu.make_async_remote_copy(
            src_ref=src, dst_ref=dst, send_sem=send, recv_sem=recv,
            device_id=device, device_id_type=MESH,
        )

    def start(copies):
        for c in copies:
            c.start()

    def arrive(copies):
        for c in copies:
            c.wait_recv()

    loads = [pltpu.make_async_copy(q_in.at[i], q.at[i], load_sem.at[i]) for i in range(FL)]
    gas_loads = [
        pltpu.make_async_copy(r, gas_own.at[i], load_sem.at[FL + 1 + i])
        for i, r in enumerate((vel_in, dif_in, mix_in))
    ]
    other_loads = [
        pltpu.make_async_copy(w_in, w, load_sem.at[FL]),
        pltpu.make_async_copy(rate_in, rate, load_sem.at[FL + 4]),
        pltpu.make_async_copy(equil_in, equil, load_sem.at[FL + 5]),
    ]

    barrier = pltpu.get_barrier_semaphore()
    first_slab = 1 - jnp.minimum(a, 1)

    def greet(device):
        pl.semaphore_signal(barrier, inc=1, device_id=device, device_id_type=MESH)

    for k in range(1, 8):
        greet((peer(k), a))
    pl.when(a != n_az - 1)(lambda: greet(dev_up))
    pl.when(a != 0)(lambda: greet(dev_dn))
    for c in gas_loads + loads + other_loads:
        c.start()
    pl.semaphore_wait(barrier, 9 - first_slab)
    pl.when(a == 0)(lambda: greet(dev_dn))
    pl.when(a == n_az - 1)(lambda: greet(dev_up))

    for c in gas_loads:
        c.wait()
    gas_sends = [
        remote(gas_own, gas.at[:, :, chunk(f)], gas_s.at[k], gas_r.at[k], (peer(k + 1), a))
        for k in range(7)
    ]
    start(gas_sends)
    gas[:, :, chunk(f)] = gas_own[...]

    halo1 = [
        remote(q_in.at[:, :, pl.ds(ROWS - 1, 1), :], h1.at[0], h1_s.at[0], h1_r.at[0], dev_up),
        remote(q_in.at[:, :, pl.ds(0, 1), :], h1.at[1], h1_s.at[1], h1_r.at[1], dev_dn),
    ]
    halo1[0].start()
    pl.when(a != 0)(lambda: halo1[1].start())

    def late_halo():
        def send():
            pl.semaphore_wait(barrier, 1)
            halo1[1].start()

        pl.when(a == 0)(send)

    def part(p):
        return pl.ds(p * HALF, HALF)

    def red(n, p, i, src, dst, device):
        return remote(src, dst, red_s.at[n * 2 + p, i], red_r.at[n * 2 + p, i], device)

    def scatter(n, p, i):
        k, device = around[i]
        return red(n, p, i, sums.at[n, part(p), :, quarter(k)], got.at[n, p, i], device)

    def exchange(n, p):
        return red(n, p, 3, sums.at[n, part(p), :, quarter(y)], got_x.at[n, p], dev_x)

    def gather(n, p, i):
        piece = total.at[n, part(p), :, quarter(y)]
        return red(n, p, 4 + i, piece, piece, around[i][1])

    def after_scatter(n, p):
        arrive([scatter(n, p, i) for i in range(3)])

        def add(i, _):
            cols = quarter(y)
            sums[n, p * HALF + i, :, cols] += got[n, p, 0, i] + (got[n, p, 1, i] + got[n, p, 2, i])
            return 0

        loop(0, HALF, add, 0)
        exchange(n, p).start()

    def after_exchange(n, p):
        exchange(n, p).wait_recv()

        def add(i, _):
            for j in range(2):
                cols, part_cols = chunk(2 * y + j), pl.ds(j * CHUNK, CHUNK)
                for t in range(2):
                    v = sums[n, p * HALF + i, tiles[t], cols] + got_x[n, p, i, tiles[t], part_cols]
                    if n == 1:
                        edge = corr[t, p * HALF + i, :, cols]
                        for k in range(7):
                            edge = edge + corr_got[k, t, p * HALF + i, :, part_cols]
                        v = v + jnp.where((first, last)[t], jnp.broadcast_to(edge, (8, CHUNK)), 0.0)
                    total[n, p * HALF + i, tiles[t], cols] = v
            return 0

        loop(0, HALF, add, 0)
        start([gather(n, p, i) for i in range(3)])

    row = lax.broadcasted_iota(jnp.int32, (8, CHUNK), 0)
    first, last = row == 0, row == 7
    tiles = (pl.ds(0, 8), pl.ds(8, 8))

    def sum_q(k):
        def body(s, _):
            acc = q[0, s, :, quarter(k)]
            for i in range(1, FL):
                acc = acc + q[i, s, :, quarter(k)]
            sums[0, s, :, quarter(k)] = acc
            return 0

        loop(0, NS, body, 0)

    for c in loads:
        c.wait()
    for i, (k, _) in enumerate(around):
        sum_q(k)
        start([scatter(0, p, i) for p in range(2)])
    sum_q(y)

    def neighbours(lower, upper, below, above):
        lower_up, upper_up = pltpu.roll(lower, 7, 0), pltpu.roll(upper, 7, 0)
        lower_dn, upper_dn = pltpu.roll(lower, 1, 0), pltpu.roll(upper, 1, 0)
        up = (jnp.where(last, upper_up, lower_up), jnp.where(last, above, upper_up))
        dn = (jnp.where(first, below, lower_dn), jnp.where(first, lower_dn, upper_dn))
        return up, dn

    def coefficients(cols, t):
        vel, dif, mix = gas[0, tiles[t], cols], gas[1, tiles[t], cols], gas[2, tiles[t], cols]
        keep = 1.0 - (2.0 * DT) * dif - (0.5 * DT) * mix
        return keep, DT * dif, (-0.5 * DT) * vel, 0.5 * jnp.sqrt(2.0 * dif)

    def burn(x):
        heating = 1.0 + 0.5 * x * x
        return DT * jnp.exp(1.0 - 1.0 / heating)

    zero = jnp.zeros((8, CHUNK), jnp.float32)

    def explicit(k):
        def column(j, _):
            cols = chunk(k * 2 + j)
            co = [coefficients(cols, t) for t in range(2)]

            def field(i, acc):
                grad_c = [co[t][2] + co[t][3] * w[i, tiles[t], cols] for t in range(2)]
                b = [burn(q[i, 0, tiles[t], cols]) for t in range(2)]
                out = []
                for s in range(NS):
                    x = [q[i, s, tiles[t], cols] for t in range(2)]
                    up, dn = neighbours(x[0], x[1], zero, zero)
                    for t in range(2):
                        v = (
                            x[t] * co[t][0]
                            + (up[t] - dn[t]) * grad_c[t]
                            + (up[t] + dn[t]) * co[t][1]
                            + (rate[s] * b[t]) * (equil[s] - x[t])
                        )
                        u[i, s, tiles[t], cols] = v
                        out.append(acc[2 * s + t] + v)
                return tuple(out)

            acc = loop(0, FL, field, (zero,) * (2 * NS))
            for s in range(NS):
                for t in range(2):
                    sums[1, s, tiles[t], cols] = acc[2 * s + t]
            return 0

        loop(0, 2, column, 0)

    def edges():
        def column(j, _):
            cols = chunk(j)
            co = [coefficients(cols, t) for t in range(2)]

            def field(i, acc):
                grad_c = [co[t][2] + co[t][3] * w[i, tiles[t], cols] for t in range(2)]
                coef = (jnp.where(first, co[0][1] - grad_c[0], 0.0), jnp.where(last, co[1][1] + grad_c[1], 0.0))
                out = []
                for s in range(NS):
                    for t in range(2):
                        v = jnp.broadcast_to(h1[t, i, s, :, cols], (8, CHUNK)) * coef[t]
                        u[i, s, tiles[t], cols] += v
                        out.append(acc[2 * s + t] + v)
                return tuple(out)

            acc = loop(0, FL, field, (zero,) * (2 * NS))
            for s in range(NS):
                corr[0, s, :, cols] = acc[2 * s][0:1]
                corr[1, s, :, cols] = acc[2 * s + 1][7:8]
            return 0

        loop(0, CELLS // CHUNK, column, 0)

    def corrections():
        out = []
        for k in range(7):
            owner = peer(k + 1)
            piece = corr.at[:, :, :, quarter(owner // 2)]
            out.append(remote(piece, corr_got.at[k], cor_s.at[k], cor_r.at[k], (owner, a)))
        return out

    halo2 = [
        remote(u.at[:, :, pl.ds(ROWS - 1, 1), :], h2.at[0], h2_s.at[0], h2_r.at[0], dev_up),
        remote(u.at[:, :, pl.ds(0, 1), :], h2.at[1], h2_s.at[1], h2_r.at[1], dev_dn),
    ]

    def mean_rows(p):
        return [
            remote(e1.at[part(p), pl.ds(ROWS - 1, 1), :], eh.at[0, part(p)], eh_s.at[0, p], eh_r.at[0, p], dev_up),
            remote(e1.at[part(p), pl.ds(0, 1), :], eh.at[1, part(p)], eh_s.at[1, p], eh_r.at[1, p], dev_dn),
        ]

    def mixing(p):
        arrive([gather(0, p, i) for i in range(3)])

        def body(i, _):
            e1[p * HALF + i] = (0.5 * DT / NF) * gas[2] * total[0, p * HALF + i]
            return 0

        loop(0, HALF, body, 0)
        start(mean_rows(p))

    def second(k, scalars):
        def column(j, _):
            cols = chunk(k * 2 + j)
            half = [tuple(0.5 * c for c in coefficients(cols, t)) for t in range(2)]
            for s in scalars:
                for t in range(2):
                    m = (0.25 * DT) * gas[2, tiles[t], cols]
                    e2[s, tiles[t], :] = m * ((1.0 / NF) * total[1, s, tiles[t], cols] + e1[s, tiles[t], cols])

            def field(i, acc):
                grad_c = [half[t][2] + half[t][3] * w[i, tiles[t], cols] for t in range(2)]
                b = [0.5 * burn(u[i, 0, tiles[t], cols] + e1[0, tiles[t], cols]) for t in range(2)]
                out = list(acc)
                for s in scalars:
                    x = [u[i, s, tiles[t], cols] + e1[s, tiles[t], cols] for t in range(2)]
                    below = jnp.broadcast_to(h2[0, i, s, :, cols] + eh[0, s, :, cols], (8, CHUNK))
                    above = jnp.broadcast_to(h2[1, i, s, :, cols] + eh[1, s, :, cols], (8, CHUNK))
                    up, dn = neighbours(x[0], x[1], below, above)
                    for t in range(2):
                        v = (
                            0.5 * q[i, s, tiles[t], cols]
                            + x[t] * half[t][0]
                            + (up[t] - dn[t]) * grad_c[t]
                            + (up[t] + dn[t]) * half[t][1]
                            + e2[s, tiles[t], :]
                            + (rate[s] * b[t]) * (equil[s] - x[t])
                        )
                        adv_out[i, s, tiles[t], cols] = v
                        if s == 0:
                            out[t] = out[t] + (1.0 + 0.5 * v * v)
                return tuple(out)

            acc = loop(0, FL, field, (zero,) * 2)
            if 0 in scalars:
                for t in range(2):
                    heat[tiles[t], cols] = acc[t]
            return 0

        loop(0, 2, column, 0)

    def den(k, n):
        out = []
        for side in range(2 if n else 1):
            owner = k * 2 + ((xl + side) % 2 if n else 1 - xl)
            out.append(
                remote(heat.at[:, chunk(owner)], heat_got.at[n, side], den_s.at[n, side], den_r.at[n, side], (owner, a))
            )
        return out

    arrive(gas_sends)
    for c in other_loads:
        c.wait()
    for i, (k, _) in enumerate(around):
        explicit(k)
        start([scatter(1, p, i) for p in range(2)])
    after_scatter(0, 0)
    after_scatter(0, 1)
    explicit(y)
    late_halo()
    arrive(halo1)
    edges()
    start(corrections())
    after_scatter(1, 0)
    after_scatter(1, 1)
    start(halo2)
    after_exchange(0, 0)
    after_exchange(0, 1)
    mixing(0)
    mixing(1)
    arrive(corrections())
    after_exchange(1, 0)
    after_exchange(1, 1)
    arrive(halo2)
    for p in range(2):
        scalars = tuple(range(p * HALF, p * HALF + HALF))
        arrive(mean_rows(p))
        for n, (k, i) in enumerate(((y, None), (yp, 2), (ym, 1), (yo, 0))):
            if n:
                gather(1, p, i).wait_recv()
            second(k, scalars)
            if p == 0:
                start(den(k, n))

    heat_sum = heat[:, chunk(f)]
    for n, k in enumerate((y, yp, ym, yo)):
        for i, c in enumerate(den(k, n)):
            c.wait_recv()
            heat_sum = heat_sum + heat_got[n, i]
    den_out[...] = 1.0 / (heat_sum * (1.0 / NF))

    for n, k in enumerate((y, yp, ym, yo)):
        for c in den(k, n):
            c.wait_send()
    for c in gas_sends + halo1 + halo2 + mean_rows(0) + mean_rows(1) + corrections():
        c.wait_send()
    for n in range(2):
        for p in range(2):
            for c in [scatter(n, p, i) for i in range(3)] + [exchange(n, p)] + [gather(n, p, i) for i in range(3)]:
                c.wait_send()


def solution(mesh):
    n_az = mesh.shape["azim"]

    def shards(scalars, wiener, velocity, diffusivity, mix_rate, reaction_rate, equilibrium):
        hbm = pl.BlockSpec(memory_space=pltpu.HBM)
        vmem = pl.BlockSpec(memory_space=pltpu.VMEM)
        f32 = jnp.float32
        dma = pltpu.SemaphoreType.DMA
        return pl.pallas_call(
            functools.partial(kernel, n_az),
            out_shape=(
                jax.ShapeDtypeStruct((FL, NS, ROWS, CELLS), f32),
                jax.ShapeDtypeStruct((ROWS, CHUNK), f32),
            ),
            in_specs=[hbm] * 7,
            out_specs=(vmem, vmem),
            scratch_shapes=[
                pltpu.VMEM((FL, NS, ROWS, CELLS), f32),
                pltpu.VMEM((FL, NS, ROWS, CELLS), f32),
                pltpu.VMEM((FL, ROWS, CELLS), f32),
                pltpu.VMEM((3, ROWS, CELLS), f32),
                pltpu.VMEM((3, ROWS, CHUNK), f32),
                pltpu.VMEM((2, FL, NS, 1, CELLS), f32),
                pltpu.VMEM((2, FL, NS, 1, CELLS), f32),
                pltpu.VMEM((2, NS, 1, CELLS), f32),
                pltpu.VMEM((2, NS, ROWS, CELLS), f32),
                pltpu.VMEM((2, 2, 3, HALF, ROWS, QUARTER), f32),
                pltpu.VMEM((2, 2, HALF, ROWS, QUARTER), f32),
                pltpu.VMEM((2, NS, ROWS, CELLS), f32),
                pltpu.VMEM((2, NS, 1, CELLS), f32),
                pltpu.VMEM((7, 2, NS, 1, QUARTER), f32),
                pltpu.VMEM((NS, ROWS, CELLS), f32),
                pltpu.VMEM((NS, ROWS, CHUNK), f32),
                pltpu.VMEM((ROWS, CELLS), f32),
                pltpu.VMEM((4, 2, ROWS, CHUNK), f32),
                pltpu.SMEM((NS,), f32),
                pltpu.SMEM((NS,), f32),
                dma((FL + 6,)),
                dma((7,)), dma((7,)),
                dma((2,)), dma((2,)),
                dma((2,)), dma((2,)),
                dma((2, 2)), dma((2, 2)),
                dma((4, 7)), dma((4, 7)),
                dma((7,)), dma((7,)),
                dma((4, 2)), dma((4, 2)),
            ],
            compiler_params=pltpu.CompilerParams(
                collective_id=0, has_side_effects=True, vmem_limit_bytes=48 << 20
            ),
            name="fields_step",
        )(
            *(
                pltpu.with_memory_space_constraint(x, pltpu.HBM)
                for x in (scalars, wiener, velocity, diffusivity, mix_rate, reaction_rate, equilibrium)
            )
        )

    return jax.shard_map(
        shards,
        mesh=mesh,
        in_specs=(
            P("field", None, "azim", None),
            P("field", "azim", None),
            P("azim", "field"),
            P("azim", "field"),
            P("azim", "field"),
            P(),
            P(),
        ),
        out_specs=(P("field", None, "azim", None), P("azim", "field")),
        check_vma=False,
    )
```

```python
import functools

import jax
import jax.numpy as jnp
from jax import lax
from jax.experimental import pallas as pl
from jax.experimental.pallas import tpu as pltpu
from jax.sharding import PartitionSpec as P

MESH = pl.DeviceIdType.MESH
loop = lax.fori_loop
NF = 64
DT = 0.2
FL = 8
NS = 10
ROWS = 16
CELLS = 1024
QUARTER = 256
CHUNK = 128
HALF = NS // 2


def kernel(
    n_az,
    q_in, w_in, vel_in, dif_in, mix_in, rate_in, equil_in,
    adv_out, den_out,
    q, u, w, gas, gas_own, h1, h2, eh, sums, got, got_x, total, corr, corr_got, e1, e2, heat, heat_got, rate, equil,
    load_sem, gas_s, gas_r, h1_s, h1_r, h2_s, h2_r, eh_s, eh_r, red_s, red_r, cor_s, cor_r, den_s, den_r,
):
    f = lax.axis_index("field")
    a = lax.axis_index("azim")
    y, xl = f // 2, f % 2
    yp, yo, ym = (y + 1) % 4, (y + 2) % 4, (y + 3) % 4
    dev_p, dev_m, dev_o, dev_x = (yp * 2 + xl, a), (ym * 2 + xl, a), (yo * 2 + xl, a), (y * 2 + 1 - xl, a)
    around = ((yo, dev_o), (yp, dev_p), (ym, dev_m))
    dev_up, dev_dn = (f, (a + 1) % n_az), (f, (a + n_az - 1) % n_az)

    def peer(k):
        return (f + k) % 8

    def chunk(i):
        return pl.ds(pl.multiple_of(i * CHUNK, CHUNK), CHUNK)

    def quarter(i):
        return pl.ds(pl.multiple_of(i * QUARTER, QUARTER), QUARTER)

    def remote(src, dst, send, recv, device):
        return pltpu.make_async_remote_copy(
            src_ref=src, dst_ref=dst, send_sem=send, recv_sem=recv,
            device_id=device, device_id_type=MESH,
        )

    def start(copies):
        for c in copies:
            c.start()

    def arrive(copies):
        for c in copies:
            c.wait_recv()

    loads = [pltpu.make_async_copy(q_in.at[i], q.at[i], load_sem.at[i]) for i in range(FL)]
    gas_loads = [
        pltpu.make_async_copy(r, gas_own.at[i], load_sem.at[FL + 1 + i])
        for i, r in enumerate((vel_in, dif_in, mix_in))
    ]
    other_loads = [
        pltpu.make_async_copy(w_in, w, load_sem.at[FL]),
        pltpu.make_async_copy(rate_in, rate, load_sem.at[FL + 4]),
        pltpu.make_async_copy(equil_in, equil, load_sem.at[FL + 5]),
    ]

    barrier = pltpu.get_barrier_semaphore()
    first_slab = 1 - jnp.minimum(a, 1)

    def greet(device):
        pl.semaphore_signal(barrier, inc=1, device_id=device, device_id_type=MESH)

    for k in range(1, 8):
        greet((peer(k), a))
    pl.when(a != n_az - 1)(lambda: greet(dev_up))
    pl.when(a != 0)(lambda: greet(dev_dn))
    for c in gas_loads + loads + other_loads:
        c.start()
    pl.semaphore_wait(barrier, 9 - first_slab)
    pl.when(a == 0)(lambda: greet(dev_dn))
    pl.when(a == n_az - 1)(lambda: greet(dev_up))

    for c in gas_loads:
        c.wait()
    gas_sends = [
        remote(gas_own, gas.at[:, :, chunk(f)], gas_s.at[k], gas_r.at[k], (peer(k + 1), a))
        for k in range(7)
    ]
    start(gas_sends)
    gas[:, :, chunk(f)] = gas_own[...]

    halo1 = [
        remote(q_in.at[:, :, pl.ds(ROWS - 1, 1), :], h1.at[0], h1_s.at[0], h1_r.at[0], dev_up),
        remote(q_in.at[:, :, pl.ds(0, 1), :], h1.at[1], h1_s.at[1], h1_r.at[1], dev_dn),
    ]
    halo1[0].start()
    pl.when(a != 0)(lambda: halo1[1].start())

    def late_halo():
        def send():
            pl.semaphore_wait(barrier, 1)
            halo1[1].start()

        pl.when(a == 0)(send)

    def part(p):
        return pl.ds(p * HALF, HALF)

    def red(n, p, i, src, dst, device):
        return remote(src, dst, red_s.at[n * 2 + p, i], red_r.at[n * 2 + p, i], device)

    def scatter(n, p, i):
        k, device = around[i]
        return red(n, p, i, sums.at[n, part(p), :, quarter(k)], got.at[n, p, i], device)

    def exchange(n, p):
        return red(n, p, 3, sums.at[n, part(p), :, quarter(y)], got_x.at[n, p], dev_x)

    def gather(n, p, i):
        piece = total.at[n, part(p), :, quarter(y)]
        return red(n, p, 4 + i, piece, piece, around[i][1])

    def after_scatter(n, p):
        arrive([scatter(n, p, i) for i in range(3)])

        def add(i, _):
            cols = quarter(y)
            sums[n, p * HALF + i, :, cols] += got[n, p, 0, i] + (got[n, p, 1, i] + got[n, p, 2, i])
            return 0

        loop(0, HALF, add, 0)
        exchange(n, p).start()

    def after_exchange(n, p):
        exchange(n, p).wait_recv()

        def add(i, _):
            for j in range(2):
                cols, part_cols = chunk(2 * y + j), pl.ds(j * CHUNK, CHUNK)
                for t in range(2):
                    v = sums[n, p * HALF + i, tiles[t], cols] + got_x[n, p, i, tiles[t], part_cols]
                    if n == 1:
                        edge = corr[t, p * HALF + i, :, cols]
                        for k in range(7):
                            edge = edge + corr_got[k, t, p * HALF + i, :, part_cols]
                        v = v + jnp.where((first, last)[t], jnp.broadcast_to(edge, (8, CHUNK)), 0.0)
                    total[n, p * HALF + i, tiles[t], cols] = v
            return 0

        loop(0, HALF, add, 0)
        start([gather(n, p, i) for i in range(3)])

    row = lax.broadcasted_iota(jnp.int32, (8, CHUNK), 0)
    first, last = row == 0, row == 7
    tiles = (pl.ds(0, 8), pl.ds(8, 8))

    def sum_q(k):
        def body(s, _):
            acc = q[0, s, :, quarter(k)]
            for i in range(1, FL):
                acc = acc + q[i, s, :, quarter(k)]
            sums[0, s, :, quarter(k)] = acc
            return 0

        loop(0, NS, body, 0)

    for c in loads:
        c.wait()
    for i, (k, _) in enumerate(around):
        sum_q(k)
        start([scatter(0, p, i) for p in range(2)])
    sum_q(y)

    def neighbours(lower, upper, below, above):
        lower_up, upper_up = pltpu.roll(lower, 7, 0), pltpu.roll(upper, 7, 0)
        lower_dn, upper_dn = pltpu.roll(lower, 1, 0), pltpu.roll(upper, 1, 0)
        up = (jnp.where(last, upper_up, lower_up), jnp.where(last, above, upper_up))
        dn = (jnp.where(first, below, lower_dn), jnp.where(first, lower_dn, upper_dn))
        return up, dn

    def coefficients(cols, t):
        vel, dif, mix = gas[0, tiles[t], cols], gas[1, tiles[t], cols], gas[2, tiles[t], cols]
        keep = 1.0 - (2.0 * DT) * dif - (0.5 * DT) * mix
        return keep, DT * dif, (-0.5 * DT) * vel, 0.5 * jnp.sqrt(2.0 * dif)

    def burn(x):
        heating = 1.0 + 0.5 * x * x
        return DT * jnp.exp(1.0 - 1.0 / heating)

    zero = jnp.zeros((8, CHUNK), jnp.float32)

    def explicit(k):
        def column(j, _):
            cols = chunk(k * 2 + j)
            co = [coefficients(cols, t) for t in range(2)]

            def field(i, acc):
                grad_c = [co[t][2] + co[t][3] * w[i, tiles[t], cols] for t in range(2)]
                b = [burn(q[i, 0, tiles[t], cols]) for t in range(2)]
                out = []
                for s in range(NS):
                    x = [q[i, s, tiles[t], cols] for t in range(2)]
                    up, dn = neighbours(x[0], x[1], zero, zero)
                    for t in range(2):
                        v = (
                            x[t] * co[t][0]
                            + (up[t] - dn[t]) * grad_c[t]
                            + (up[t] + dn[t]) * co[t][1]
                            + (rate[s] * b[t]) * (equil[s] - x[t])
                        )
                        u[i, s, tiles[t], cols] = v
                        out.append(acc[2 * s + t] + v)
                return tuple(out)

            acc = loop(0, FL, field, (zero,) * (2 * NS))
            for s in range(NS):
                for t in range(2):
                    sums[1, s, tiles[t], cols] = acc[2 * s + t]
            return 0

        loop(0, 2, column, 0)

    def edges():
        def column(j, _):
            cols = chunk(j)
            co = [coefficients(cols, t) for t in range(2)]

            def field(i, acc):
                grad_c = [co[t][2] + co[t][3] * w[i, tiles[t], cols] for t in range(2)]
                coef = (jnp.where(first, co[0][1] - grad_c[0], 0.0), jnp.where(last, co[1][1] + grad_c[1], 0.0))
                out = []
                for s in range(NS):
                    for t in range(2):
                        v = jnp.broadcast_to(h1[t, i, s, :, cols], (8, CHUNK)) * coef[t]
                        u[i, s, tiles[t], cols] += v
                        out.append(acc[2 * s + t] + v)
                return tuple(out)

            acc = loop(0, FL, field, (zero,) * (2 * NS))
            for s in range(NS):
                corr[0, s, :, cols] = acc[2 * s][0:1]
                corr[1, s, :, cols] = acc[2 * s + 1][7:8]
            return 0

        loop(0, CELLS // CHUNK, column, 0)

    def corrections():
        out = []
        for k in range(7):
            owner = peer(k + 1)
            piece = corr.at[:, :, :, quarter(owner // 2)]
            out.append(remote(piece, corr_got.at[k], cor_s.at[k], cor_r.at[k], (owner, a)))
        return out

    halo2 = [
        remote(u.at[:, :, pl.ds(ROWS - 1, 1), :], h2.at[0], h2_s.at[0], h2_r.at[0], dev_up),
        remote(u.at[:, :, pl.ds(0, 1), :], h2.at[1], h2_s.at[1], h2_r.at[1], dev_dn),
    ]

    def mean_rows(p):
        return [
            remote(e1.at[part(p), pl.ds(ROWS - 1, 1), :], eh.at[0, part(p)], eh_s.at[0, p], eh_r.at[0, p], dev_up),
            remote(e1.at[part(p), pl.ds(0, 1), :], eh.at[1, part(p)], eh_s.at[1, p], eh_r.at[1, p], dev_dn),
        ]

    def mixing(p):
        arrive([gather(0, p, i) for i in range(3)])

        def body(i, _):
            e1[p * HALF + i] = (0.5 * DT / NF) * gas[2] * total[0, p * HALF + i]
            return 0

        loop(0, HALF, body, 0)
        start(mean_rows(p))

    def second(k, scalars):
        def column(j, _):
            cols = chunk(k * 2 + j)
            half = [tuple(0.5 * c for c in coefficients(cols, t)) for t in range(2)]
            for s in scalars:
                for t in range(2):
                    m = (0.25 * DT) * gas[2, tiles[t], cols]
                    e2[s, tiles[t], :] = m * ((1.0 / NF) * total[1, s, tiles[t], cols] + e1[s, tiles[t], cols])

            def field(i, acc):
                grad_c = [half[t][2] + half[t][3] * w[i, tiles[t], cols] for t in range(2)]
                b = [0.5 * burn(u[i, 0, tiles[t], cols] + e1[0, tiles[t], cols]) for t in range(2)]
                out = list(acc)
                for s in scalars:
                    x = [u[i, s, tiles[t], cols] + e1[s, tiles[t], cols] for t in range(2)]
                    below = jnp.broadcast_to(h2[0, i, s, :, cols] + eh[0, s, :, cols], (8, CHUNK))
                    above = jnp.broadcast_to(h2[1, i, s, :, cols] + eh[1, s, :, cols], (8, CHUNK))
                    up, dn = neighbours(x[0], x[1], below, above)
                    for t in range(2):
                        v = (
                            0.5 * q[i, s, tiles[t], cols]
                            + x[t] * half[t][0]
                            + (up[t] - dn[t]) * grad_c[t]
                            + (up[t] + dn[t]) * half[t][1]
                            + e2[s, tiles[t], :]
                            + (rate[s] * b[t]) * (equil[s] - x[t])
                        )
                        adv_out[i, s, tiles[t], cols] = v
                        if s == 0:
                            out[t] = out[t] + (1.0 + 0.5 * v * v)
                return tuple(out)

            acc = loop(0, FL, field, (zero,) * 2)
            if 0 in scalars:
                for t in range(2):
                    heat[tiles[t], cols] = acc[t]
            return 0

        loop(0, 2, column, 0)

    def den(k, n):
        out = []
        for side in range(2 if n else 1):
            owner = k * 2 + ((xl + side) % 2 if n else 1 - xl)
            out.append(
                remote(heat.at[:, chunk(owner)], heat_got.at[n, side], den_s.at[n, side], den_r.at[n, side], (owner, a))
            )
        return out

    arrive(gas_sends)
    for c in other_loads:
        c.wait()
    for i, (k, _) in enumerate(around):
        explicit(k)
        start([scatter(1, p, i) for p in range(2)])
    after_scatter(0, 0)
    after_scatter(0, 1)
    explicit(y)
    late_halo()
    arrive(halo1)
    edges()
    start(corrections())
    after_scatter(1, 0)
    after_scatter(1, 1)
    start(halo2)
    after_exchange(0, 0)
    after_exchange(0, 1)
    mixing(0)
    mixing(1)
    arrive(corrections())
    after_exchange(1, 0)
    after_exchange(1, 1)
    arrive(halo2)
    parts = [tuple(range(p * HALF, p * HALF + HALF)) for p in range(2)]
    arrive(mean_rows(0))
    second(y, parts[0])
    start(den(y, 0))
    arrive(mean_rows(1))
    second(y, parts[1])
    for p in range(2):
        for n, (k, i) in enumerate(((yp, 2), (ym, 1), (yo, 0))):
            gather(1, p, i).wait_recv()
            second(k, parts[p])
            if p == 0:
                start(den(k, n + 1))

    heat_sum = heat[:, chunk(f)]
    for n, k in enumerate((y, yp, ym, yo)):
        for i, c in enumerate(den(k, n)):
            c.wait_recv()
            heat_sum = heat_sum + heat_got[n, i]
    den_out[...] = 1.0 / (heat_sum * (1.0 / NF))

    for n, k in enumerate((y, yp, ym, yo)):
        for c in den(k, n):
            c.wait_send()
    for c in gas_sends + halo1 + halo2 + mean_rows(0) + mean_rows(1) + corrections():
        c.wait_send()
    for n in range(2):
        for p in range(2):
            for c in [scatter(n, p, i) for i in range(3)] + [exchange(n, p)] + [gather(n, p, i) for i in range(3)]:
                c.wait_send()


def solution(mesh):
    n_az = mesh.shape["azim"]

    def shards(scalars, wiener, velocity, diffusivity, mix_rate, reaction_rate, equilibrium):
        hbm = pl.BlockSpec(memory_space=pltpu.HBM)
        vmem = pl.BlockSpec(memory_space=pltpu.VMEM)
        f32 = jnp.float32
        dma = pltpu.SemaphoreType.DMA
        return pl.pallas_call(
            functools.partial(kernel, n_az),
            out_shape=(
                jax.ShapeDtypeStruct((FL, NS, ROWS, CELLS), f32),
                jax.ShapeDtypeStruct((ROWS, CHUNK), f32),
            ),
            in_specs=[hbm] * 7,
            out_specs=(vmem, vmem),
            scratch_shapes=[
                pltpu.VMEM((FL, NS, ROWS, CELLS), f32),
                pltpu.VMEM((FL, NS, ROWS, CELLS), f32),
                pltpu.VMEM((FL, ROWS, CELLS), f32),
                pltpu.VMEM((3, ROWS, CELLS), f32),
                pltpu.VMEM((3, ROWS, CHUNK), f32),
                pltpu.VMEM((2, FL, NS, 1, CELLS), f32),
                pltpu.VMEM((2, FL, NS, 1, CELLS), f32),
                pltpu.VMEM((2, NS, 1, CELLS), f32),
                pltpu.VMEM((2, NS, ROWS, CELLS), f32),
                pltpu.VMEM((2, 2, 3, HALF, ROWS, QUARTER), f32),
                pltpu.VMEM((2, 2, HALF, ROWS, QUARTER), f32),
                pltpu.VMEM((2, NS, ROWS, CELLS), f32),
                pltpu.VMEM((2, NS, 1, CELLS), f32),
                pltpu.VMEM((7, 2, NS, 1, QUARTER), f32),
                pltpu.VMEM((NS, ROWS, CELLS), f32),
                pltpu.VMEM((NS, ROWS, CHUNK), f32),
                pltpu.VMEM((ROWS, CELLS), f32),
                pltpu.VMEM((4, 2, ROWS, CHUNK), f32),
                pltpu.SMEM((NS,), f32),
                pltpu.SMEM((NS,), f32),
                dma((FL + 6,)),
                dma((7,)), dma((7,)),
                dma((2,)), dma((2,)),
                dma((2,)), dma((2,)),
                dma((2, 2)), dma((2, 2)),
                dma((4, 7)), dma((4, 7)),
                dma((7,)), dma((7,)),
                dma((4, 2)), dma((4, 2)),
            ],
            compiler_params=pltpu.CompilerParams(
                collective_id=0, has_side_effects=True, vmem_limit_bytes=48 << 20
            ),
            name="fields_step",
        )(
            *(
                pltpu.with_memory_space_constraint(x, pltpu.HBM)
                for x in (scalars, wiener, velocity, diffusivity, mix_rate, reaction_rate, equilibrium)
            )
        )

    return jax.shard_map(
        shards,
        mesh=mesh,
        in_specs=(
            P("field", None, "azim", None),
            P("field", "azim", None),
            P("azim", "field"),
            P("azim", "field"),
            P("azim", "field"),
            P(),
            P(),
        ),
        out_specs=(P("field", None, "azim", None), P("azim", "field")),
        check_vma=False,
    )
```
